32 devices in a mesh: freq: 4 (over x, core), tile: 8 (over z, y).
Axes of the slice: x: 2, y: 2, z: 4, core: 2. Of those that a mesh axis runs over, the one named last changes fastest.
Arguments:
- plus_time: bfloat16 [128, 128, 12288], P('freq', None, 'tile'), may hold values from -6 to 6
- minus_time: bfloat16 [128, 128, 12288], P('freq', None, 'tile'), may hold values from -6 to 6
- gate_starts: int32 [128, 48], P('freq', 'tile'), may hold values from 0 to 64
- tile_ranks: int32 [4, 48, 48], P('freq', None, 'tile'), may hold values from 1 to 64, as said below
- u_factors: bfloat16 [4, 48, 48, 2, 64, 256], P('freq', 'tile'), may hold values from -0.109375 to 0.109375
- v_factors: bfloat16 [4, 48, 48, 2, 64, 256], P('freq', None, 'tile'), may hold values from -0.375 to 0.375
Outputs:
- minus_new: bfloat16 [4, 2, 128, 12288], P('freq', None, None, 'tile')
- plus_new: bfloat16 [4, 2, 128, 12288], P('freq', None, None, 'tile')
- cross_gram: float32 [4, 2, 128, 128], P('freq', None, 'tile')
- normal_gram: float32 [4, 2, 128, 128], P('freq', None, 'tile')
The draws below stay inside these ranges and needn't reach their ends.
Inputs may be any that keep to these rules, and one draw needn't show every extreme that they name: `tile_ranks`: tiles with |i - j| <= 1 have rank 64; every other tile has rank at most 32, and some tile of every draw has exactly 32.
All inputs are finite; a program needn't handle non-finite values.
Results may differ from the reference program's by a relative error of at most 0.014.
Values may be sent and summed in bfloat16 or wider, within the bound.
A program may use at most 192 MiB of HBM per device.

```python
import math
import jax
import jax.numpy as jnp
from jax import lax

S = 128
R = 12288
TILE = 256
KMAX = 64
GATE = 64
NSAMP = 128
NT = 48
F = 4


def draw_tile_ranks(key, part):
    base_ranks = jax.random.randint(jax.random.fold_in(key, 11), (F, NT, NT), KMAX // 4, KMAX // 2 + 1)
    row_ids = lax.broadcasted_iota(jnp.int32, (F, NT, NT), 1)
    col_ids = lax.broadcasted_iota(jnp.int32, (F, NT, NT), 2)
    near_diag = jnp.abs(row_ids - col_ids) <= 1
    corner = (row_ids == 0) & (col_ids == NT - 1)
    base_ranks = jnp.where(corner, KMAX // 2, base_ranks)
    return jnp.where(near_diag, KMAX, base_ranks).astype(jnp.int32)


def set_ends(result, key, smallest, largest):
    place = [jax.random.randint(jax.random.fold_in(key, axis), (), 0, length) for axis, length in enumerate(result.shape)]
    main_axis = result.shape.index(max(result.shape))
    neighbour = place[:main_axis] + [(place[main_axis] + 1) % result.shape[main_axis]] + place[main_axis + 1:]
    return result.at[tuple(place)].set(smallest).at[tuple(neighbour)].set(largest)


def block_scale(stream_key, shape, shards, low, high):
    gain, own = 1.0, jax.random.fold_in(stream_key, 6)
    for axis_at, shards_of in shards:
        draws = jnp.exp(jax.random.uniform(jax.random.fold_in(own, axis_at), (shards_of,), jnp.float32, low / len(shards), high / len(shards)))
        gain = gain * jnp.repeat(draws, shape[axis_at] // shards_of).reshape([-1 if axis == axis_at else 1 for axis in range(len(shape))])
    return gain


def scatter_about(rng, dims, width, bound, cuts=(), kind=jnp.bfloat16):
    level = block_scale(rng, dims, cuts, -0.22, 0.18) if cuts else 1.0
    values = jax.random.normal(rng, dims, jnp.float32) * width * level
    return jnp.minimum(jnp.maximum(values, -bound), bound).astype(kind)


def setup_inputs(seed: int = 0) -> dict:
    arg_keys = jax.random.split(jax.random.key(seed), 7)
    plus_time = scatter_about(arg_keys[0], (S, NSAMP, R), 1.0, 6.0, ((0, 4), (2, 8)))
    minus_time = scatter_about(arg_keys[1], (S, NSAMP, R), 1.0, 6.0, ((0, 4), (2, 8)))
    gate_starts = set_ends(jax.random.randint(arg_keys[2], (S, NT), 0, NSAMP - GATE + 1), jax.random.fold_in(arg_keys[2], 1), 0, NSAMP - GATE).astype(jnp.int32)
    tile_ranks = draw_tile_ranks(jax.random.fold_in(arg_keys[6], 71), 0)
    u_factors = scatter_about(arg_keys[4], (F, NT, NT, 2, KMAX, TILE), (NT * KMAX) ** -0.5, 0.109375, ((0, 4), (1, 8)))
    v_factors = scatter_about(arg_keys[5], (F, NT, NT, 2, KMAX, TILE), TILE ** -0.5, 0.375, ((0, 4), (2, 8)))
    return dict(plus_time=plus_time, minus_time=minus_time, gate_starts=gate_starts, tile_ranks=tile_ranks, u_factors=u_factors, v_factors=v_factors)


def make_table(freq_count, sample_count):
    freq_ids = lax.broadcasted_iota(jnp.int32, (freq_count, sample_count), 0)
    sample_ids = lax.broadcasted_iota(jnp.int32, (freq_count, sample_count), 1)
    phase_ids = freq_ids * sample_ids % sample_count
    angles = phase_ids.astype(jnp.float32) * (2.0 * math.pi / sample_count)
    amplitude = 1.0 / math.sqrt(GATE)
    return jnp.stack([jnp.cos(angles) * amplitude, -jnp.sin(angles) * amplitude]).astype(jnp.bfloat16)

def half_signs(entry_count):
    entry_ids = lax.broadcasted_iota(jnp.int32, (entry_count,), 0)
    return jnp.where(entry_ids < entry_count // 2, 1.0, -1.0).astype(jnp.float32)

def reference(plus_time, minus_time, gate_starts, tile_ranks, u_factors, v_factors):
    tile_count = R // TILE
    dft_table = make_table(F, NSAMP)
    flat_table = dft_table.reshape(2 * F, NSAMP)

    def one_source(src_items):
        plus_row, minus_row, gate_row = src_items
        starts = jnp.repeat(gate_row, TILE)[None, :]
        sample_ids = jnp.arange(NSAMP, dtype=jnp.int32)[:, None]
        inside = (sample_ids >= starts) & (sample_ids < starts + GATE)
        zero_val = jnp.zeros((), plus_row.dtype)
        plus_spec = jnp.dot(flat_table, jnp.where(inside, plus_row, zero_val), preferred_element_type=jnp.float32)
        minus_spec = jnp.dot(flat_table, jnp.where(inside, minus_row, zero_val), preferred_element_type=jnp.float32)
        return jnp.stack([plus_spec, minus_spec]).reshape(2, 2, F, R)
    per_source = lax.map(one_source, (plus_time, minus_time, gate_starts))
    spectra = jnp.transpose(per_source, (3, 2, 1, 0, 4)).astype(jnp.bfloat16)
    sign_vec = half_signs(2 * S)
    rank_ids = jnp.arange(KMAX, dtype=jnp.int32)

    def one_freq(freq_items):
        spec_freq, u_freq, v_freq, rank_freq = freq_items
        columns = spec_freq.reshape(2, 2 * S, tile_count, TILE).astype(jnp.float32)

        def one_row(row_items):
            u_row, v_row, ranks_row = row_items
            partial_c = jnp.einsum('jckr,dsjr->jcdks', v_row.astype(jnp.float32), columns, precision=lax.Precision.HIGHEST)
            coeff_real = partial_c[:, 0, 0] - sign_vec * partial_c[:, 1, 1]
            coeff_imag = partial_c[:, 0, 1] + sign_vec * partial_c[:, 1, 0]
            rank_mask = (rank_ids[None, :] < ranks_row[:, None]).astype(jnp.float32)[:, :, None]
            coeff_all = jnp.stack([coeff_real * rank_mask, coeff_imag * rank_mask], 1).astype(jnp.bfloat16)
            products = jnp.einsum('jckr,jeks->cesr', u_row.astype(jnp.float32), coeff_all.astype(jnp.float32), precision=lax.Precision.HIGHEST)
            resp_real = products[0, 0] - sign_vec[:, None] * products[1, 1]
            resp_imag = products[0, 1] + sign_vec[:, None] * products[1, 0]
            return jnp.stack([resp_real, resp_imag])
        rows_out = lax.map(one_row, (u_freq, v_freq, rank_freq))
        return jnp.transpose(rows_out, (1, 2, 0, 3)).reshape(2, 2 * S, R)
    response = lax.map(one_freq, (spectra, u_factors, v_factors, tile_ranks))
    rounded = response.astype(jnp.bfloat16)
    minus_new = rounded[:, :, :S]
    plus_new = rounded[:, :, S:]
    gram_parts = jnp.einsum('fczr,fesr->fczes', rounded.astype(jnp.float32), plus_new.astype(jnp.float32), precision=lax.Precision.HIGHEST)
    gram_real = gram_parts[:, 0, :, 0] + gram_parts[:, 1, :, 1]
    gram_imag = gram_parts[:, 1, :, 0] - gram_parts[:, 0, :, 1]
    cross_gram = jnp.stack([gram_real[:, :S], gram_imag[:, :S]], 1) / math.sqrt(R)
    normal_gram = jnp.stack([gram_real[:, S:], gram_imag[:, S:]], 1) / R
    return (minus_new, plus_new, cross_gram, normal_gram)
```

```python
import functools
import math

import jax
import jax.numpy as jnp
from jax import lax
from jax.experimental import pallas as pl
from jax.experimental.pallas import tpu as pltpu
from jax.sharding import PartitionSpec as P

GATE = 64
MESH = pl.DeviceIdType.MESH
NT_DIMS = (((1,), (1,)), ((), ()))
TN_DIMS = (((0,), (0,)), ((), ()))


def make_table(freq_count, sample_count):
    freq_ids = lax.broadcasted_iota(jnp.int32, (freq_count, sample_count), 0)
    sample_ids = lax.broadcasted_iota(jnp.int32, (freq_count, sample_count), 1)
    phase_ids = freq_ids * sample_ids % sample_count
    angles = phase_ids.astype(jnp.float32) * (2.0 * math.pi / sample_count)
    amplitude = 1.0 / math.sqrt(GATE)
    return jnp.stack([jnp.cos(angles) * amplitude, -jnp.sin(angles) * amplitude]).astype(
        jnp.bfloat16
    )


def gate_table(freq_total, samples):
    table = make_table(freq_total, samples).transpose(1, 0, 2).astype(jnp.float32)
    table = table.reshape(freq_total * 2, samples)
    return jnp.concatenate([table, table], axis=1)


def partner(me, step, n):
    other, bit = 0, 1
    while bit < n:
        other = other + bit * ((me // bit + step // bit) % 2)
        bit *= 2
    return other


def swapped(block, count, axis):
    parts = [lax.slice_in_dim(block, n * count, (n + 1) * count, axis=axis) for n in range(4)]
    return jnp.concatenate([-parts[2], parts[3], parts[0], -parts[1]], axis=axis)


def operator_kernel(
    n, nf, starts_hbm, ranks_hbm, table_hbm, plus_hbm, minus_hbm, u_hbm, v_hbm,
    minus, plus, cross, normal,
    starts, ranks, small, table, spec, traces, xall, v_s, u_s, vb, ub, send, recv, cband, bin_,
    acc, gsum, gsend, grecv,
    sem_s, sem_t, sem_v, sem_u, sem_vb, sem_ub, fsend, frecv, csend, crecv, rsend, rrecv,
    bsend, brecv, gs_sem, gr_sem,
):
    me = lax.axis_index("tile")
    mf = lax.axis_index("freq")
    tiles, half, width = v_s.shape[0], v_s.shape[3], v_s.shape[4]
    sl = spec.shape[3]
    count = sl * nf
    lanes = 4 * count
    base = me * tiles
    total_tiles = n * tiles
    samples = traces.shape[3]
    rows = table.shape[0]
    sources = rows // (2 * nf)
    blocks = sl // sources
    first = 1 - (me + n - 1) // n
    last = (me + 1) // n
    inner = ((me + n // 4) // (n // 2)) % 2

    def load_v(j):
        return pltpu.make_async_copy(
            v_hbm.at[0, :, j, :, pl.ds(0, half), :], v_s.at[j], sem_v.at[j]
        )

    def load_u(m):
        src = partner(me, m, n)
        return pltpu.make_async_copy(
            u_hbm.at[0, :, pl.ds(src * tiles, tiles), :, pl.ds(0, half), :],
            u_s.at[:, pl.ds(m * tiles, tiles)],
            sem_u.at[m],
        )

    def load_band(o, j, right):
        row, col = base + j + o - 1, base + j - o + 1
        if j + o - 1 < 0:
            row = row + first
        if j + o - 1 >= tiles:
            row = row - last
        if j - o + 1 < 0:
            col = col + first
        if j - o + 1 >= tiles:
            col = col - last
        if right:
            return pltpu.make_async_copy(
                v_hbm.at[0, row, j, :, pl.ds(half, half), :], vb.at[o, j], sem_vb.at[o, j]
            )
        return pltpu.make_async_copy(
            u_hbm.at[0, j, col, :, pl.ds(half, half), :], ub.at[o, j], sem_ub.at[o, j]
        )

    def columns(j):
        return pl.ds(pl.multiple_of(j * width, width), width)

    def freq_copy(g, j, block):
        peer = partner(mf, g, nf)
        part = pl.ds(block * sources, sources)
        place = pl.ds(pl.multiple_of(mf * sl + block * sources, sources), sources)
        return pltpu.make_async_remote_copy(
            src_ref=spec.at[peer, :, :, part, columns(j)],
            dst_ref=xall.at[:, :, place, columns(j)],
            send_sem=fsend.at[g, j, block],
            recv_sem=frecv.at[g, j, block],
            device_id={"freq": peer},
            device_id_type=MESH,
        )

    def slots(m, j, size):
        return pl.ds((m * tiles + j) * half, size * half)

    def first_copy(m):
        return pltpu.make_async_remote_copy(
            src_ref=send.at[m, :, pl.ds(0, half)],
            dst_ref=recv.at[:, slots(m, 0, 1)],
            send_sem=csend.at[m],
            recv_sem=crecv.at[m],
            device_id={"tile": partner(me, m, n)},
            device_id_type=MESH,
        )

    def row_copy(m, i):
        return pltpu.make_async_remote_copy(
            src_ref=send.at[m, i, pl.ds(half, (tiles - 1) * half)],
            dst_ref=recv.at[i, slots(m, 1, tiles - 1)],
            send_sem=rsend.at[m, i],
            recv_sem=rrecv.at[m, i],
            device_id={"tile": partner(me, m, n)},
            device_id_type=MESH,
        )

    def band_copy(side):
        source = cband.at[2, tiles + 1] if side == 0 else cband.at[0, 0]
        target = lax.rem(me + 1, n) if side == 0 else lax.rem(me + n - 1, n)
        return pltpu.make_async_remote_copy(
            src_ref=source,
            dst_ref=bin_.at[side],
            send_sem=bsend.at[side],
            recv_sem=brecv.at[side],
            device_id={"tile": target},
            device_id_type=MESH,
        )

    def gram_copy(m):
        other = partner(me, m, n)
        return pltpu.make_async_remote_copy(
            src_ref=gsend.at[other],
            dst_ref=grecv.at[m],
            send_sem=gs_sem.at[m],
            recv_sem=gr_sem.at[m],
            device_id={"tile": other},
            device_id_type=MESH,
        )

    def load_traces(q, j, block):
        source = minus_hbm if q else plus_hbm
        part = pl.ds(block * sources, sources)
        return pltpu.make_async_copy(
            source.at[part, :, columns(j)], traces.at[j % 2, q, part], sem_t.at[q, j, block]
        )

    barrier = pltpu.get_barrier_semaphore()
    for m in range(1, n):
        pl.semaphore_signal(
            barrier, inc=1, device_id={"tile": partner(me, m, n)}, device_id_type=MESH
        )
    for g in range(1, nf):
        pl.semaphore_signal(
            barrier, inc=1, device_id={"freq": partner(mf, g, nf)}, device_id_type=MESH
        )

    small_copies = [
        pltpu.make_async_copy(table_hbm, small, sem_s.at[0]),
        pltpu.make_async_copy(starts_hbm, starts, sem_s.at[1]),
        pltpu.make_async_copy(ranks_hbm, ranks, sem_s.at[2]),
    ]
    for copy in small_copies:
        copy.start()
    for j in range(min(2, tiles)):
        for block in range(blocks):
            for q in range(2):
                load_traces(q, j, block).start()
        load_v(j).start()
        if j == 0:
            for o in range(3):
                for jj in range(tiles):
                    load_band(o, jj, True).start()

    shape = (2 * nf, sources, 2 * samples)
    row_source = lax.broadcasted_iota(jnp.int32, shape, 1).reshape(rows, 2 * samples)
    column = lax.broadcasted_iota(jnp.int32, (rows, 2 * samples), 1)
    second = column >= samples
    sample = jnp.where(second, column - samples, column)
    row_source = row_source - second.astype(jnp.int32)
    for copy in small_copies:
        copy.wait()
    table[...] = jnp.broadcast_to(small[...][:, None, :], shape).reshape(rows, 2 * samples)

    def own_rows(block):
        return pl.ds(pl.multiple_of(mf * sl + block * sources, sources), sources)

    def spectra(j, block):
        for q in range(2):
            load_traces(q, j, block).wait()
        totals = [jnp.zeros((rows, width), jnp.float32) for _ in range(2)]
        for pair in range(sources // 2):
            first_id = block * sources + 2 * pair
            start = jnp.where(second, starts[j, first_id + 1], starts[j, first_id])
            inside = (sample >= start) & (sample < start + GATE) & (row_source == 2 * pair)
            gated = jnp.where(inside, table[...], 0.0).astype(jnp.bfloat16)
            for q in range(2):
                values = traces[j % 2, q, first_id : first_id + 2]
                totals[q] += jnp.dot(
                    gated,
                    values.reshape(2 * samples, width),
                    preferred_element_type=jnp.float32,
                )
        part = slice(block * sources, (block + 1) * sources)
        for q in range(2):
            spec[:, :, q, part, columns(j)] = (
                totals[q].reshape(nf, 2, sources, width).astype(jnp.bfloat16)
            )

    def share_spectra(j, block):
        for g in range(nf - 1, 0, -1):
            freq_copy(g, j, block).start()
        part = slice(block * sources, (block + 1) * sources)
        xall[:, :, own_rows(block), columns(j)] = spec[mf, :, :, part, columns(j)]

    rank_id = lax.broadcasted_iota(jnp.int32, (half, lanes), 0)

    def product(a_real, a_imag, b_one, b_two):
        return lax.dot_general(
            a_real, b_one, NT_DIMS, preferred_element_type=jnp.float32
        ) + lax.dot_general(a_imag, b_two, NT_DIMS, preferred_element_type=jnp.float32)

    def coefficients(j, leading):
        for block in range(blocks):
            for g in range(1, nf):
                freq_copy(g, j, block).wait_recv()
        load_v(j).wait()
        b_one = xall[:, :, :, columns(j)].reshape(lanes, width)
        b_two = swapped(b_one, count, 0)

        def tile_block(m, own):
            row = partner(me, m, n) * tiles
            c = product(
                v_s[j, pl.ds(row, tiles), 0].reshape(tiles * half, width),
                v_s[j, pl.ds(row, tiles), 1].reshape(tiles * half, width),
                b_one,
                b_two,
            )
            for i in range(tiles):
                kept = jnp.where(
                    rank_id < ranks[j, 0, row + i], c[i * half : (i + 1) * half], 0.0
                ).astype(jnp.bfloat16)
                if own:
                    recv[i, slots(m, j, 1)] = kept
                else:
                    send[m, i, pl.ds(j * half, half)] = kept

        for k in range(n - 1):
            m = k + 1
            if leading:
                near = k + n // 2 if k < n // 2 else k - n // 2 + 1
                m = inner * near + (1 - inner) * m
            tile_block(m, False)
            if leading:
                first_copy(m).start()
        tile_block(0, True)

        for o in range(3):
            load_band_wait(o, j)
        c = product(
            vb[:, j, 0].reshape(3 * half, width), vb[:, j, 1].reshape(3 * half, width), b_one, b_two
        ).astype(jnp.bfloat16)
        for o in range(3):
            cband[o, j + o] = c[o * half : (o + 1) * half]

    def load_band_wait(o, j):
        pltpu.make_async_copy(
            v_hbm.at[0, 0, j, :, pl.ds(half, half), :], vb.at[o, j], sem_vb.at[o, j]
        ).wait()

    for block in range(blocks):
        spectra(0, block)
        if block == 0:
            pl.semaphore_wait(barrier, n + nf - 2)
        share_spectra(0, block)
    if tiles > 2:
        for block in range(blocks):
            for q in range(2):
                load_traces(q, 2, block).start()
    for block in range(blocks):
        spectra(1, block)
        share_spectra(1, block)
    if tiles > 3:
        for block in range(blocks):
            for q in range(2):
                load_traces(q, 3, block).start()
    for j in range(2, tiles):
        load_v(j).start()
    coefficients(0, True)
    band_copy(1).start()
    for m in range(n):
        load_u(m).start()
    for j in range(tiles):
        for o in range(3):
            load_band(o, j, False).start()

    def advance(step, _):
        @pl.when(step < tiles)
        def _():
            for block in range(blocks):
                spectra(step, block)
                share_spectra(step, block)

        @pl.when(step + 2 < tiles)
        def _():
            for block in range(blocks):
                for q in range(2):
                    load_traces(q, step + 2, block).start()

        coefficients(step - 1, False)
        return 0

    lax.fori_loop(2, tiles + 1, advance, 0)

    def send_rows(i, _):
        for m in range(1, n):
            row_copy(m, i).start()
        return 0

    band_copy(0).start()
    lax.fori_loop(0, tiles, send_rows, 0)

    for m in range(n):
        load_u(m).wait()
    for j in range(tiles):
        for o in range(3):
            load_band(o, j, False).wait()
    for m in range(1, n):
        first_copy(m).wait_recv()
    band_copy(0).wait_recv()
    band_copy(1).wait_recv()
    zero = jnp.zeros((half, lanes), jnp.bfloat16)
    bin_[0] = jnp.where(first == 0, bin_[0], zero)
    bin_[1] = jnp.where(last == 0, bin_[1], zero)
    cband[2, 0 + 1] = bin_[0]
    cband[0, tiles] = bin_[1]
    gsum[...] = jnp.zeros_like(gsum)

    def transposed(c, u):
        return lax.dot_general(c, u, TN_DIMS, preferred_element_type=jnp.float32)

    def add_source(m, i):
        c = recv[i, slots(m, 0, tiles)]
        for part in range(2):
            u = u_s[i, pl.ds(m * tiles, tiles), part].reshape(tiles * half, width)
            acc[part] += transposed(c, u)

    def respond(i, _):
        c = jnp.concatenate([cband[o, i + 1] for o in range(3)], axis=0)
        for part in range(2):
            acc[part] = transposed(c, ub[:, i, part].reshape(3 * half, width))
        add_source(0, i)

        def from_peer(m, _):
            row_copy(m, i).wait_recv()
            add_source(m, i)
            return 0

        lax.fori_loop(1, n, from_peer, 0)
        parts = []
        for p, (other, sign) in enumerate(((2, -1), (3, 1), (0, 1), (1, -1))):
            one = acc[0, p * count : (p + 1) * count]
            two = acc[1, other * count : (other + 1) * count]
            parts.append((one + two if sign > 0 else one - two).astype(jnp.bfloat16))
        for c in range(2):
            minus[0, c, :, columns(i)] = parts[2 * c]
            plus[0, c, :, columns(i)] = parts[2 * c + 1]
        gsum[...] += lax.dot_general(
            jnp.concatenate(parts, axis=0),
            jnp.concatenate([parts[1], parts[3]], axis=0),
            NT_DIMS,
            preferred_element_type=jnp.float32,
        )
        return 0

    lax.fori_loop(0, tiles, respond, 0)

    receivers = total_tiles * width
    share = count // n
    outs = (cross, normal)
    for q, scale in enumerate((1.0 / math.sqrt(receivers), 1.0 / receivers)):
        top = slice(q * count, (q + 1) * count)
        low = slice((2 + q) * count, (3 + q) * count)
        real = (gsum[top, :count] + gsum[low, count:]) * scale
        imag = (gsum[low, :count] - gsum[top, count:]) * scale
        for d in range(n):
            gsend[d, q, 0] = real[d * share : (d + 1) * share].astype(jnp.bfloat16)
            gsend[d, q, 1] = imag[d * share : (d + 1) * share].astype(jnp.bfloat16)
    for m in range(n - 1, 0, -1):
        gram_copy(m).start()
    for q, scale in enumerate((1.0 / math.sqrt(receivers), 1.0 / receivers)):
        mine = pl.ds(pl.multiple_of(q * count + me * share, share), share)
        under = pl.ds(pl.multiple_of((2 + q) * count + me * share, share), share)
        outs[q][0, 0] = (gsum[mine, :count] + gsum[under, count:]) * scale
        outs[q][0, 1] = (gsum[under, :count] - gsum[mine, count:]) * scale
    for m in range(1, n):
        gram_copy(m).wait_recv()
        for q in range(2):
            outs[q][0] += grecv[m, q].astype(jnp.float32)

    for j in range(tiles):
        for block in range(blocks):
            for g in range(1, nf):
                freq_copy(g, j, block).wait_send()
        for m in range(1, n):
            row_copy(m, j).wait_send()
    for m in range(1, n):
        first_copy(m).wait_send()
    band_copy(0).wait_send()
    band_copy(1).wait_send()
    for m in range(1, n):
        gram_copy(m).wait_send()


def hand_over(count, *refs):
    copies = [
        pltpu.make_async_copy(refs[k], refs[count + k], refs[2 * count].at[k]) for k in range(count)
    ]
    for copy in copies:
        copy.start()
    for copy in copies:
        copy.wait()


def on_device(n, nf, plus_time, minus_time, gate_starts, tile_ranks, u_factors, v_factors):
    freq_total = u_factors.shape[0] * nf
    tiles = v_factors.shape[2]
    half = v_factors.shape[4] // 2
    width = v_factors.shape[5]
    sl, samples, receivers = plus_time.shape
    table = gate_table(freq_total, samples)
    sources = math.gcd(16, sl)
    blocks = sl // sources
    rows = freq_total * 2 * sources
    count = sl * nf
    lanes = 4 * count
    share = count // n
    bf16, f32 = jnp.bfloat16, jnp.float32
    vmem = pl.BlockSpec(memory_space=pltpu.VMEM)
    anywhere = pl.BlockSpec(memory_space=pl.ANY)
    dma = pltpu.SemaphoreType.DMA
    starts = gate_starts.T
    ranks = tile_ranks.transpose(2, 0, 1)
    shapes = (
            jax.ShapeDtypeStruct((1, 2, count, receivers), bf16),
            jax.ShapeDtypeStruct((1, 2, count, receivers), bf16),
            jax.ShapeDtypeStruct((1, 2, share, count), f32),
            jax.ShapeDtypeStruct((1, 2, share, count), f32),
    )
    results = pl.pallas_call(
        functools.partial(operator_kernel, n, nf),
        out_shape=tuple(pltpu.VMEM(shape.shape, shape.dtype) for shape in shapes),
        in_specs=[anywhere] * 7,
        out_specs=(vmem, vmem, vmem, vmem),
        scratch_shapes=[
            pltpu.SMEM(starts.shape, jnp.int32),
            pltpu.SMEM(ranks.shape, jnp.int32),
            pltpu.VMEM(table.shape, f32),
            pltpu.VMEM((rows, 2 * samples), f32),
            pltpu.VMEM((freq_total, 2, 2, sl, receivers), bf16),
            pltpu.VMEM((2, 2, sl, samples, width), bf16),
            pltpu.VMEM((2, 2, count, receivers), bf16),
            pltpu.VMEM((tiles, n * tiles, 2, half, width), bf16),
            pltpu.VMEM((tiles, n * tiles, 2, half, width), bf16),
            pltpu.VMEM((3, tiles, 2, half, width), bf16),
            pltpu.VMEM((3, tiles, 2, half, width), bf16),
            pltpu.VMEM((n, tiles, tiles * half, lanes), bf16),
            pltpu.VMEM((tiles, n * tiles * half, lanes), bf16),
            pltpu.VMEM((3, tiles + 2, half, lanes), bf16),
            pltpu.VMEM((2, half, lanes), bf16),
            pltpu.VMEM((2, lanes, width), f32),
            pltpu.VMEM((lanes, 2 * count), f32),
            pltpu.VMEM((n, 2, 2, share, count), bf16),
            pltpu.VMEM((n, 2, 2, share, count), bf16),
            dma((3,)),
            dma((2, tiles, blocks)),
            dma((tiles,)),
            dma((n,)),
            dma((3, tiles)),
            dma((3, tiles)),
            dma((nf, tiles, blocks)),
            dma((nf, tiles, blocks)),
            dma((n,)),
            dma((n,)),
            dma((n, tiles)),
            dma((n, tiles)),
            dma((2,)),
            dma((2,)),
            dma((n,)),
            dma((n,)),
        ],
        compiler_params=pltpu.CompilerParams(
            collective_id=0, has_side_effects=True, vmem_limit_bytes=57 << 20
        ),
        name="reflection_operator",
    )(starts, ranks, table, plus_time, minus_time, u_factors, v_factors)
    return pl.pallas_call(
        functools.partial(hand_over, len(shapes)),
        out_shape=shapes,
        in_specs=[vmem] * len(shapes),
        out_specs=[anywhere] * len(shapes),
        scratch_shapes=[dma((len(shapes),))],
        compiler_params=pltpu.CompilerParams(vmem_limit_bytes=4 << 20),
        name="hand_over",
    )(*results)


def solution(mesh):
    placed = (
        P("freq", None, "tile"),
        P("freq", None, "tile"),
        P("freq", "tile"),
        P("freq", None, "tile"),
        P("freq", "tile", None, None, None, None),
        P("freq", None, "tile", None, None, None),
    )
    return jax.shard_map(
        functools.partial(on_device, mesh.shape["tile"], mesh.shape["freq"]),
        mesh=mesh,
        in_specs=placed,
        out_specs=(
            P("freq", None, None, "tile"),
            P("freq", None, None, "tile"),
            P("freq", None, "tile", None),
            P("freq", None, "tile", None),
        ),
        check_vma=False,
    )
```

```python
import functools
import math

import jax
import jax.numpy as jnp
import numpy as np
from jax import lax
from jax.experimental import pallas as pl
from jax.experimental.pallas import tpu as pltpu
from jax.sharding import PartitionSpec as P

GATE = 64
MESH = pl.DeviceIdType.MESH
NT_DIMS = (((1,), (1,)), ((), ()))
TN_DIMS = (((0,), (0,)), ((), ()))


def gate_table(freq_count, sample_count):
    phase_ids = np.arange(freq_count)[:, None] * np.arange(sample_count)[None] % sample_count
    angles = phase_ids.astype(np.float32) * np.float32(2.0 * math.pi / sample_count)
    amplitude = np.float32(1.0 / math.sqrt(GATE))
    table = np.stack([np.cos(angles) * amplitude, -np.sin(angles) * amplitude], axis=1)
    table = table.reshape(freq_count * 2, sample_count).astype(jnp.bfloat16).astype(np.float32)
    return np.concatenate([table, table], axis=1)


def partner(me, step, n):
    other, bit = 0, 1
    while bit < n:
        other = other + bit * ((me // bit + step // bit) % 2)
        bit *= 2
    return other


def swapped(block, count, axis):
    parts = [lax.slice_in_dim(block, n * count, (n + 1) * count, axis=axis) for n in range(4)]
    return jnp.concatenate([-parts[2], parts[3], parts[0], -parts[1]], axis=axis)


def operator_kernel(
    n, nf, starts_hbm, ranks_hbm, table_hbm, plus_hbm, minus_hbm, u_hbm, v_hbm,
    minus, plus, cross, normal,
    starts, ranks, small, table, spec, traces, xall, v_s, u_s, vb, ub, send, recv, cband, bin_,
    acc, gsum, gsend, grecv,
    sem_s, sem_t, sem_v, sem_u, sem_vb, sem_ub, fsend, frecv, csend, crecv, rsend, rrecv,
    bsend, brecv, gs_sem, gr_sem,
):
    me = lax.axis_index("tile")
    mf = lax.axis_index("freq")
    tiles, half, width = v_s.shape[0], v_s.shape[3], v_s.shape[4]
    sl = spec.shape[3]
    count = sl * nf
    lanes = 4 * count
    groups = xall.shape[0]
    near = nf // groups
    chunk = near * sl
    group_lanes = 4 * chunk
    base = me * tiles
    total_tiles = n * tiles
    samples = traces.shape[3]
    rows = table.shape[0]
    sources = rows // (2 * nf)
    blocks = sl // sources
    first = 1 - (me + n - 1) // n
    last = (me + 1) // n
    inner = ((me + n // 4) // (n // 2)) % 2

    def load_v(j):
        return pltpu.make_async_copy(
            v_hbm.at[0, :, j, :, pl.ds(0, half), :], v_s.at[j], sem_v.at[j]
        )

    def load_u(m):
        src = partner(me, m, n)
        return pltpu.make_async_copy(
            u_hbm.at[0, :, pl.ds(src * tiles, tiles), :, pl.ds(0, half), :],
            u_s.at[:, pl.ds(m * tiles, tiles)],
            sem_u.at[m],
        )

    def load_band(o, j, right):
        row, col = base + j + o - 1, base + j - o + 1
        if j + o - 1 < 0:
            row = row + first
        if j + o - 1 >= tiles:
            row = row - last
        if j - o + 1 < 0:
            col = col + first
        if j - o + 1 >= tiles:
            col = col - last
        if right:
            return pltpu.make_async_copy(
                v_hbm.at[0, row, j, :, pl.ds(half, half), :], vb.at[o, j], sem_vb.at[o, j]
            )
        return pltpu.make_async_copy(
            u_hbm.at[0, j, col, :, pl.ds(half, half), :], ub.at[o, j], sem_ub.at[o, j]
        )

    def columns(j):
        return pl.ds(pl.multiple_of(j * width, width), width)

    def own_rows(block):
        return pl.ds(pl.multiple_of(mf % near * sl + block * sources, sources), sources)

    def freq_copy(g, j, block):
        peer = partner(mf, g, nf)
        part = pl.ds(block * sources, sources)
        return pltpu.make_async_remote_copy(
            src_ref=spec.at[peer, :, :, part, columns(j)],
            dst_ref=xall.at[mf // near, :, :, own_rows(block), columns(j)],
            send_sem=fsend.at[g, j, block],
            recv_sem=frecv.at[g, j, block],
            device_id={"freq": peer},
            device_id_type=MESH,
        )

    def slots(m, j, size):
        return pl.ds((m * tiles + j) * half, size * half)

    def first_copy(m, d):
        h = partner(mf // near, d, groups)
        return pltpu.make_async_remote_copy(
            src_ref=send.at[h, m, :, pl.ds(0, half)],
            dst_ref=recv.at[h, :, slots(m, 0, 1)],
            send_sem=csend.at[m, d],
            recv_sem=crecv.at[m, d],
            device_id={"tile": partner(me, m, n)},
            device_id_type=MESH,
        )

    def row_copy(m, i, h):
        return pltpu.make_async_remote_copy(
            src_ref=send.at[h, m, i, pl.ds(half, (tiles - 1) * half)],
            dst_ref=recv.at[h, i, slots(m, 1, tiles - 1)],
            send_sem=rsend.at[m, i, h],
            recv_sem=rrecv.at[m, i, h],
            device_id={"tile": partner(me, m, n)},
            device_id_type=MESH,
        )

    def band_copy(side):
        source = cband.at[2, tiles + 1] if side == 0 else cband.at[0, 0]
        target = lax.rem(me + 1, n) if side == 0 else lax.rem(me + n - 1, n)
        return pltpu.make_async_remote_copy(
            src_ref=source,
            dst_ref=bin_.at[side],
            send_sem=bsend.at[side],
            recv_sem=brecv.at[side],
            device_id={"tile": target},
            device_id_type=MESH,
        )

    def gram_copy(m):
        other = partner(me, m, n)
        return pltpu.make_async_remote_copy(
            src_ref=gsend.at[other],
            dst_ref=grecv.at[m],
            send_sem=gs_sem.at[m],
            recv_sem=gr_sem.at[m],
            device_id={"tile": other},
            device_id_type=MESH,
        )

    def load_traces(q, j, block):
        source = minus_hbm if q else plus_hbm
        part = pl.ds(block * sources, sources)
        return pltpu.make_async_copy(
            source.at[part, :, columns(j)], traces.at[j % 2, q, part], sem_t.at[q, j, block]
        )

    barrier = pltpu.get_barrier_semaphore()
    for m in range(1, n):
        pl.semaphore_signal(
            barrier, inc=1, device_id={"tile": partner(me, m, n)}, device_id_type=MESH
        )
    for g in range(1, nf):
        pl.semaphore_signal(
            barrier, inc=1, device_id={"freq": partner(mf, g, nf)}, device_id_type=MESH
        )

    small_copies = [
        pltpu.make_async_copy(table_hbm, small, sem_s.at[0]),
        pltpu.make_async_copy(starts_hbm, starts, sem_s.at[1]),
        pltpu.make_async_copy(ranks_hbm, ranks, sem_s.at[2]),
    ]
    for copy in small_copies:
        copy.start()
    for j in range(min(2, tiles)):
        for block in range(blocks):
            for q in range(2):
                load_traces(q, j, block).start()
        load_v(j).start()
        if j == 0:
            for o in range(3):
                for jj in range(tiles):
                    load_band(o, jj, True).start()

    shape = (2 * nf, sources, 2 * samples)
    row_source = lax.broadcasted_iota(jnp.int32, shape, 1).reshape(rows, 2 * samples)
    column = lax.broadcasted_iota(jnp.int32, (rows, 2 * samples), 1)
    second = column >= samples
    sample = jnp.where(second, column - samples, column)
    row_source = row_source - second.astype(jnp.int32)
    for copy in small_copies:
        copy.wait()
    table[...] = jnp.broadcast_to(small[...][:, None, :], shape).reshape(rows, 2 * samples)

    def spectra(j, block):
        for q in range(2):
            load_traces(q, j, block).wait()
        totals = [jnp.zeros((rows, width), jnp.float32) for _ in range(2)]
        for pair in range(sources // 2):
            first_id = block * sources + 2 * pair
            start = jnp.where(second, starts[j, first_id + 1], starts[j, first_id])
            inside = (sample >= start) & (sample < start + GATE) & (row_source == 2 * pair)
            gated = jnp.where(inside, table[...], 0.0).astype(jnp.bfloat16)
            for q in range(2):
                values = traces[j % 2, q, first_id : first_id + 2]
                totals[q] += jnp.dot(
                    gated,
                    values.reshape(2 * samples, width),
                    preferred_element_type=jnp.float32,
                )
        part = slice(block * sources, (block + 1) * sources)
        for q in range(2):
            spec[:, :, q, part, columns(j)] = (
                totals[q].reshape(nf, 2, sources, width).astype(jnp.bfloat16)
            )

    def share_spectra(j, block):
        for g in range(1, nf):
            freq_copy(g, j, block).start()
        part = slice(block * sources, (block + 1) * sources)
        xall[mf // near, :, :, own_rows(block), columns(j)] = spec[mf, :, :, part, columns(j)]

    def product(a_real, a_imag, b_one, b_two):
        return lax.dot_general(
            a_real, b_one, NT_DIMS, preferred_element_type=jnp.float32
        ) + lax.dot_general(a_imag, b_two, NT_DIMS, preferred_element_type=jnp.float32)

    def tile_block(m, j, b_one, b_two, halves, own):
        row = partner(me, m, n) * tiles
        rank_id = lax.broadcasted_iota(jnp.int32, (half, b_one.shape[0]), 0)
        c = product(
            v_s[j, pl.ds(row, tiles), 0].reshape(tiles * half, width),
            v_s[j, pl.ds(row, tiles), 1].reshape(tiles * half, width),
            b_one,
            b_two,
        )
        for i in range(tiles):
            kept = jnp.where(
                rank_id < ranks[j, 0, row + i], c[i * half : (i + 1) * half], 0.0
            ).astype(jnp.bfloat16)
            for at, h in enumerate(halves):
                piece = kept[:, at * group_lanes : (at + 1) * group_lanes]
                if own:
                    recv[h, i, slots(m, j, 1)] = piece
                else:
                    send[h, m, i, pl.ds(j * half, half)] = piece

    def first_coefficients(d):
        for block in range(blocks):
            for g in range(max(1, d * near), (d + 1) * near):
                freq_copy(g, 0, block).wait_recv()
        h = partner(mf // near, d, groups)
        b_one = xall[h, :, :, :, columns(0)].reshape(group_lanes, width)
        b_two = swapped(b_one, chunk, 0)
        for k in range(n - 1):
            crossing = k + n // 2 if k < n // 2 else k - n // 2 + 1
            m = inner * crossing + (1 - inner) * (k + 1)
            tile_block(m, 0, b_one, b_two, [h], False)
            first_copy(m, d).start()
        tile_block(0, 0, b_one, b_two, [h], True)

    def coefficients(j, leading):
        if not leading:
            for block in range(blocks):
                for g in range(1, nf):
                    freq_copy(g, j, block).wait_recv()
            load_v(j).wait()
        b_one = xall[:, :, :, :, columns(j)].reshape(lanes, width)
        b_two = jnp.concatenate(
            [
                swapped(b_one[h * group_lanes : (h + 1) * group_lanes], chunk, 0)
                for h in range(groups)
            ],
            axis=0,
        )
        if not leading:
            for m in range(n):
                tile_block(m, j, b_one, b_two, range(groups), m == 0)
        for o in range(3):
            load_band_wait(o, j)
        c = product(
            vb[:, j, 0].reshape(3 * half, width), vb[:, j, 1].reshape(3 * half, width), b_one, b_two
        ).astype(jnp.bfloat16)
        for o in range(3):
            cband[o, j + o] = c[o * half : (o + 1) * half]

    def load_band_wait(o, j):
        pltpu.make_async_copy(
            v_hbm.at[0, 0, j, :, pl.ds(half, half), :], vb.at[o, j], sem_vb.at[o, j]
        ).wait()

    for block in range(blocks):
        spectra(0, block)
        if block == 0:
            pl.semaphore_wait(barrier, n + nf - 2)
        share_spectra(0, block)
    if tiles > 2:
        for block in range(blocks):
            for q in range(2):
                load_traces(q, 2, block).start()
    load_v(0).wait()
    first_coefficients(0)
    for block in range(blocks):
        spectra(1, block)
        share_spectra(1, block)
    for d in range(1, groups):
        first_coefficients(d)
    if tiles > 3:
        for block in range(blocks):
            for q in range(2):
                load_traces(q, 3, block).start()
    for j in range(2, tiles):
        load_v(j).start()
    coefficients(0, True)
    band_copy(1).start()
    for m in range(n):
        load_u(m).start()
    for j in range(tiles):
        for o in range(3):
            load_band(o, j, False).start()

    def advance(step, _):
        @pl.when(step < tiles)
        def _():
            for block in range(blocks):
                spectra(step, block)
                share_spectra(step, block)

        @pl.when(step + 2 < tiles)
        def _():
            for block in range(blocks):
                for q in range(2):
                    load_traces(q, step + 2, block).start()

        coefficients(step - 1, False)
        return 0

    lax.fori_loop(2, tiles + 1, advance, 0)

    def send_rows(i, _):
        for h in range(groups):
            for m in range(1, n):
                row_copy(m, i, h).start()
        return 0

    band_copy(0).start()
    lax.fori_loop(0, tiles, send_rows, 0)

    for m in range(n):
        load_u(m).wait()
    for j in range(tiles):
        for o in range(3):
            load_band(o, j, False).wait()
    for m in range(1, n):
        for d in range(groups):
            first_copy(m, d).wait_recv()
    band_copy(0).wait_recv()
    band_copy(1).wait_recv()
    zero = jnp.zeros((half, lanes), jnp.bfloat16)
    bin_[0] = jnp.where(first == 0, bin_[0], zero)
    bin_[1] = jnp.where(last == 0, bin_[1], zero)
    cband[2, 0 + 1] = bin_[0]
    cband[0, tiles] = bin_[1]
    gsum[...] = jnp.zeros_like(gsum)

    def transposed(c, u):
        return lax.dot_general(c, u, TN_DIMS, preferred_element_type=jnp.float32)

    def add_source(m, i):
        c = jnp.concatenate([recv[h, i, slots(m, 0, tiles)] for h in range(groups)], axis=1)
        for part in range(2):
            u = u_s[i, pl.ds(m * tiles, tiles), part].reshape(tiles * half, width)
            acc[part] += transposed(c, u)

    def respond(i, _):
        c = jnp.concatenate([cband[o, i + 1] for o in range(3)], axis=0)
        for part in range(2):
            acc[part] = transposed(c, ub[:, i, part].reshape(3 * half, width))
        add_source(0, i)

        def from_peer(m, _):
            for h in range(groups):
                row_copy(m, i, h).wait_recv()
            add_source(m, i)
            return 0

        lax.fori_loop(1, n, from_peer, 0)
        parts = []
        for p, (other, sign) in enumerate(((2, -1), (3, 1), (0, 1), (1, -1))):
            blocks_of = []
            for h in range(groups):
                one = acc[0, pl.ds(h * group_lanes + p * chunk, chunk)]
                two = acc[1, pl.ds(h * group_lanes + other * chunk, chunk)]
                blocks_of.append(one + two if sign > 0 else one - two)
            parts.append(jnp.concatenate(blocks_of, axis=0).astype(jnp.bfloat16))
        for c in range(2):
            minus[0, c, :, columns(i)] = parts[2 * c]
            plus[0, c, :, columns(i)] = parts[2 * c + 1]
        gsum[...] += lax.dot_general(
            jnp.concatenate(parts, axis=0),
            jnp.concatenate([parts[1], parts[3]], axis=0),
            NT_DIMS,
            preferred_element_type=jnp.float32,
        )
        return 0

    lax.fori_loop(0, tiles, respond, 0)

    receivers = total_tiles * width
    share = count // n
    outs = (cross, normal)
    for q, scale in enumerate((1.0 / math.sqrt(receivers), 1.0 / receivers)):
        top = slice(q * count, (q + 1) * count)
        low = slice((2 + q) * count, (3 + q) * count)
        real = (gsum[top, :count] + gsum[low, count:]) * scale
        imag = (gsum[low, :count] - gsum[top, count:]) * scale
        for d in range(n):
            gsend[d, q, 0] = real[d * share : (d + 1) * share].astype(jnp.bfloat16)
            gsend[d, q, 1] = imag[d * share : (d + 1) * share].astype(jnp.bfloat16)
    for m in range(n - 1, 0, -1):
        gram_copy(m).start()
    for q, scale in enumerate((1.0 / math.sqrt(receivers), 1.0 / receivers)):
        mine = pl.ds(pl.multiple_of(q * count + me * share, share), share)
        under = pl.ds(pl.multiple_of((2 + q) * count + me * share, share), share)
        outs[q][0, 0] = (gsum[mine, :count] + gsum[under, count:]) * scale
        outs[q][0, 1] = (gsum[under, :count] - gsum[mine, count:]) * scale
    for m in range(1, n):
        gram_copy(m).wait_recv()
        for q in range(2):
            outs[q][0] += grecv[m, q].astype(jnp.float32)

    for j in range(tiles):
        for block in range(blocks):
            for g in range(1, nf):
                freq_copy(g, j, block).wait_send()
        for m in range(1, n):
            for h in range(groups):
                row_copy(m, j, h).wait_send()
    for m in range(1, n):
        for d in range(groups):
            first_copy(m, d).wait_send()
    band_copy(0).wait_send()
    band_copy(1).wait_send()
    for m in range(1, n):
        gram_copy(m).wait_send()


def hand_over(count, *refs):
    copies = [
        pltpu.make_async_copy(refs[k], refs[count + k], refs[2 * count].at[k]) for k in range(count)
    ]
    for copy in copies:
        copy.start()
    for copy in copies:
        copy.wait()


def on_device(n, nf, plus_time, minus_time, gate_starts, tile_ranks, u_factors, v_factors):
    freq_total = u_factors.shape[0] * nf
    tiles = v_factors.shape[2]
    half = v_factors.shape[4] // 2
    width = v_factors.shape[5]
    sl, samples, receivers = plus_time.shape
    table = gate_table(freq_total, samples)
    sources = math.gcd(16, sl)
    blocks = sl // sources
    rows = freq_total * 2 * sources
    count = sl * nf
    lanes = 4 * count
    share = count // n
    near = math.gcd(nf, 2)
    groups = nf // near
    bf16, f32 = jnp.bfloat16, jnp.float32
    vmem = pl.BlockSpec(memory_space=pltpu.VMEM)
    anywhere = pl.BlockSpec(memory_space=pl.ANY)
    dma = pltpu.SemaphoreType.DMA
    starts = gate_starts.T
    ranks = tile_ranks.transpose(2, 0, 1)
    shapes = (
            jax.ShapeDtypeStruct((1, 2, count, receivers), bf16),
            jax.ShapeDtypeStruct((1, 2, count, receivers), bf16),
            jax.ShapeDtypeStruct((1, 2, share, count), f32),
            jax.ShapeDtypeStruct((1, 2, share, count), f32),
    )
    results = pl.pallas_call(
        functools.partial(operator_kernel, n, nf),
        out_shape=tuple(pltpu.VMEM(shape.shape, shape.dtype) for shape in shapes),
        in_specs=[anywhere] * 7,
        out_specs=(vmem, vmem, vmem, vmem),
        scratch_shapes=[
            pltpu.SMEM(starts.shape, jnp.int32),
            pltpu.SMEM(ranks.shape, jnp.int32),
            pltpu.VMEM(table.shape, f32),
            pltpu.VMEM((rows, 2 * samples), f32),
            pltpu.VMEM((freq_total, 2, 2, sl, receivers), bf16),
            pltpu.VMEM((2, 2, sl, samples, width), bf16),
            pltpu.VMEM((groups, 2, 2, near * sl, receivers), bf16),
            pltpu.VMEM((tiles, n * tiles, 2, half, width), bf16),
            pltpu.VMEM((tiles, n * tiles, 2, half, width), bf16),
            pltpu.VMEM((3, tiles, 2, half, width), bf16),
            pltpu.VMEM((3, tiles, 2, half, width), bf16),
            pltpu.VMEM((groups, n, tiles, tiles * half, lanes // groups), bf16),
            pltpu.VMEM((groups, tiles, n * tiles * half, lanes // groups), bf16),
            pltpu.VMEM((3, tiles + 2, half, lanes), bf16),
            pltpu.VMEM((2, half, lanes), bf16),
            pltpu.VMEM((2, lanes, width), f32),
            pltpu.VMEM((lanes, 2 * count), f32),
            pltpu.VMEM((n, 2, 2, share, count), bf16),
            pltpu.VMEM((n, 2, 2, share, count), bf16),
            dma((3,)),
            dma((2, tiles, blocks)),
            dma((tiles,)),
            dma((n,)),
            dma((3, tiles)),
            dma((3, tiles)),
            dma((nf, tiles, blocks)),
            dma((nf, tiles, blocks)),
            dma((n, groups)),
            dma((n, groups)),
            dma((n, tiles, groups)),
            dma((n, tiles, groups)),
            dma((2,)),
            dma((2,)),
            dma((n,)),
            dma((n,)),
        ],
        compiler_params=pltpu.CompilerParams(
            collective_id=0, has_side_effects=True, vmem_limit_bytes=57 << 20
        ),
        name="reflection_operator",
    )(starts, ranks, table, plus_time, minus_time, u_factors, v_factors)
    return pl.pallas_call(
        functools.partial(hand_over, len(shapes)),
        out_shape=shapes,
        in_specs=[vmem] * len(shapes),
        out_specs=[anywhere] * len(shapes),
        scratch_shapes=[dma((len(shapes),))],
        compiler_params=pltpu.CompilerParams(vmem_limit_bytes=4 << 20),
        name="hand_over",
    )(*results)


def solution(mesh):
    placed = (
        P("freq", None, "tile"),
        P("freq", None, "tile"),
        P("freq", "tile"),
        P("freq", None, "tile"),
        P("freq", "tile", None, None, None, None),
        P("freq", None, "tile", None, None, None),
    )
    return jax.shard_map(
        functools.partial(on_device, mesh.shape["tile"], mesh.shape["freq"]),
        mesh=mesh,
        in_specs=placed,
        out_specs=(
            P("freq", None, None, "tile"),
            P("freq", None, None, "tile"),
            P("freq", None, "tile", None),
            P("freq", None, "tile", None),
        ),
        check_vma=False,
    )
```

```python
import functools
import math

import jax
import jax.numpy as jnp
import numpy as np
from jax import lax
from jax.experimental import pallas as pl
from jax.experimental.pallas import tpu as pltpu
from jax.sharding import PartitionSpec as P

GATE = 64
MESH = pl.DeviceIdType.MESH
NT_DIMS = (((1,), (1,)), ((), ()))
TN_DIMS = (((0,), (0,)), ((), ()))


def gate_table(freq_count, sample_count):
    phase_ids = np.arange(freq_count)[:, None] * np.arange(sample_count)[None] % sample_count
    angles = phase_ids.astype(np.float32) * np.float32(2.0 * math.pi / sample_count)
    amplitude = np.float32(1.0 / math.sqrt(GATE))
    table = np.stack([np.cos(angles) * amplitude, -np.sin(angles) * amplitude], axis=1)
    table = table.reshape(freq_count * 2, sample_count).astype(jnp.bfloat16).astype(np.float32)
    return np.concatenate([table, table], axis=1)


def partner(me, step, n):
    other, bit = 0, 1
    while bit < n:
        other = other + bit * ((me // bit + step // bit) % 2)
        bit *= 2
    return other


def swapped(block, count, axis):
    parts = [lax.slice_in_dim(block, n * count, (n + 1) * count, axis=axis) for n in range(4)]
    return jnp.concatenate([-parts[2], parts[3], parts[0], -parts[1]], axis=axis)


def operator_kernel(
    n, nf, starts_hbm, ranks_hbm, table_hbm, plus_hbm, minus_hbm, u_hbm, v_hbm,
    minus, plus, cross, normal,
    starts, ranks, small, table, spec, traces, xall, v_s, u_s, vb, ub, send, recv, cband, bin_,
    acc, gsum, gsend, grecv,
    sem_s, sem_t, sem_v, sem_u, sem_vb, sem_ub, fsend, frecv, csend, crecv, rsend, rrecv,
    bsend, brecv, gs_sem, gr_sem,
):
    me = lax.axis_index("tile")
    mf = lax.axis_index("freq")
    tiles, half, width = v_s.shape[0], v_s.shape[3], v_s.shape[4]
    sl = spec.shape[3]
    count = sl * nf
    lanes = 4 * count
    groups = xall.shape[0]
    near = nf // groups
    chunk = near * sl
    group_lanes = 4 * chunk
    core = mf % near
    base = me * tiles
    total_tiles = n * tiles
    samples = traces.shape[3]
    rows = table.shape[0]
    sources = rows // (2 * nf)
    blocks = sl // sources
    first = 1 - (me + n - 1) // n
    last = (me + 1) // n
    inner = ((me + n // 4) // (n // 2)) % 2

    def load_v(j):
        return pltpu.make_async_copy(
            v_hbm.at[0, :, j, :, pl.ds(0, half), :], v_s.at[j], sem_v.at[j]
        )

    def load_u(m):
        src = partner(me, m, n)
        return pltpu.make_async_copy(
            u_hbm.at[0, :, pl.ds(src * tiles, tiles), :, pl.ds(0, half), :],
            u_s.at[:, pl.ds(m * tiles, tiles)],
            sem_u.at[m],
        )

    def load_band(o, j, right):
        row, col = base + j + o - 1, base + j - o + 1
        if j + o - 1 < 0:
            row = row + first
        if j + o - 1 >= tiles:
            row = row - last
        if j - o + 1 < 0:
            col = col + first
        if j - o + 1 >= tiles:
            col = col - last
        if right:
            return pltpu.make_async_copy(
                v_hbm.at[0, row, j, :, pl.ds(half, half), :], vb.at[o, j], sem_vb.at[o, j]
            )
        return pltpu.make_async_copy(
            u_hbm.at[0, j, col, :, pl.ds(half, half), :], ub.at[o, j], sem_ub.at[o, j]
        )

    def columns(j):
        return pl.ds(pl.multiple_of(j * width, width), width)

    def own_rows(block):
        return pl.ds(pl.multiple_of(mf % near * sl + block * sources, sources), sources)

    def freq_copy(g, j, block):
        peer = partner(mf, g, nf)
        part = pl.ds(block * sources, sources)
        return pltpu.make_async_remote_copy(
            src_ref=spec.at[peer, :, :, part, columns(j)],
            dst_ref=xall.at[mf // near, :, :, own_rows(block), columns(j)],
            send_sem=fsend.at[g, j, block],
            recv_sem=frecv.at[g, j, block],
            device_id={"freq": peer},
            device_id_type=MESH,
        )

    def slots(m, j, size):
        return pl.ds((m * tiles + j) * half, size * half)

    def across(k):
        return n // 2 + (1 - core) * k + core * (n // 2 - 1 - k)

    def first_copy(m, d):
        h = partner(mf // near, d, groups)
        return pltpu.make_async_remote_copy(
            src_ref=send.at[h, m, :, pl.ds(0, half)],
            dst_ref=recv.at[h, :, slots(m, 0, 1)],
            send_sem=csend.at[m, d],
            recv_sem=crecv.at[m, d],
            device_id={"tile": partner(me, m, n)},
            device_id_type=MESH,
        )

    def row_copy(m, i, h):
        return pltpu.make_async_remote_copy(
            src_ref=send.at[h, m, i, pl.ds(half, (tiles - 1) * half)],
            dst_ref=recv.at[h, i, slots(m, 1, tiles - 1)],
            send_sem=rsend.at[m, i, h],
            recv_sem=rrecv.at[m, i, h],
            device_id={"tile": partner(me, m, n)},
            device_id_type=MESH,
        )

    def band_copy(side):
        source = cband.at[2, tiles + 1] if side == 0 else cband.at[0, 0]
        target = lax.rem(me + 1, n) if side == 0 else lax.rem(me + n - 1, n)
        return pltpu.make_async_remote_copy(
            src_ref=source,
            dst_ref=bin_.at[side],
            send_sem=bsend.at[side],
            recv_sem=brecv.at[side],
            device_id={"tile": target},
            device_id_type=MESH,
        )

    def gram_copy(m):
        other = partner(me, m, n)
        return pltpu.make_async_remote_copy(
            src_ref=gsend.at[other],
            dst_ref=grecv.at[m],
            send_sem=gs_sem.at[m],
            recv_sem=gr_sem.at[m],
            device_id={"tile": other},
            device_id_type=MESH,
        )

    def load_traces(q, j, block):
        source = minus_hbm if q else plus_hbm
        part = pl.ds(block * sources, sources)
        return pltpu.make_async_copy(
            source.at[part, :, columns(j)], traces.at[j % 2, q, part], sem_t.at[q, j, block]
        )

    barrier = pltpu.get_barrier_semaphore()
    for m in range(1, n):
        pl.semaphore_signal(
            barrier, inc=1, device_id={"tile": partner(me, m, n)}, device_id_type=MESH
        )
    for g in range(1, nf):
        pl.semaphore_signal(
            barrier, inc=1, device_id={"freq": partner(mf, g, nf)}, device_id_type=MESH
        )

    small_copies = [
        pltpu.make_async_copy(table_hbm, small, sem_s.at[0]),
        pltpu.make_async_copy(starts_hbm, starts, sem_s.at[1]),
        pltpu.make_async_copy(ranks_hbm, ranks, sem_s.at[2]),
    ]
    for copy in small_copies:
        copy.start()
    for j in range(min(2, tiles)):
        for block in range(blocks):
            for q in range(2):
                load_traces(q, j, block).start()
        load_v(j).start()
        if j == 0:
            for o in range(3):
                for jj in range(tiles):
                    load_band(o, jj, True).start()

    shape = (2 * nf, sources, 2 * samples)
    row_source = lax.broadcasted_iota(jnp.int32, shape, 1).reshape(rows, 2 * samples)
    column = lax.broadcasted_iota(jnp.int32, (rows, 2 * samples), 1)
    second = column >= samples
    sample = jnp.where(second, column - samples, column)
    row_source = row_source - second.astype(jnp.int32)
    for copy in small_copies:
        copy.wait()
    table[...] = jnp.broadcast_to(small[...][:, None, :], shape).reshape(rows, 2 * samples)

    def spectra(j, block):
        for q in range(2):
            load_traces(q, j, block).wait()
        totals = [jnp.zeros((rows, width), jnp.float32) for _ in range(2)]
        for pair in range(sources // 2):
            first_id = block * sources + 2 * pair
            start = jnp.where(second, starts[j, first_id + 1], starts[j, first_id])
            inside = (sample >= start) & (sample < start + GATE) & (row_source == 2 * pair)
            gated = jnp.where(inside, table[...], 0.0).astype(jnp.bfloat16)
            for q in range(2):
                values = traces[j % 2, q, first_id : first_id + 2]
                totals[q] += jnp.dot(
                    gated,
                    values.reshape(2 * samples, width),
                    preferred_element_type=jnp.float32,
                )
        part = slice(block * sources, (block + 1) * sources)
        for q in range(2):
            spec[:, :, q, part, columns(j)] = (
                totals[q].reshape(nf, 2, sources, width).astype(jnp.bfloat16)
            )

    def share_spectra(j, block):
        for g in range(1, nf):
            freq_copy(g, j, block).start()
        part = slice(block * sources, (block + 1) * sources)
        xall[mf // near, :, :, own_rows(block), columns(j)] = spec[mf, :, :, part, columns(j)]

    def product(a_real, a_imag, b_one, b_two):
        return lax.dot_general(
            a_real, b_one, NT_DIMS, preferred_element_type=jnp.float32
        ) + lax.dot_general(a_imag, b_two, NT_DIMS, preferred_element_type=jnp.float32)

    def tile_block(m, j, b_one, b_two, halves, own):
        row = partner(me, m, n) * tiles
        rank_id = lax.broadcasted_iota(jnp.int32, (half, b_one.shape[0]), 0)
        c = product(
            v_s[j, pl.ds(row, tiles), 0].reshape(tiles * half, width),
            v_s[j, pl.ds(row, tiles), 1].reshape(tiles * half, width),
            b_one,
            b_two,
        )
        for i in range(tiles):
            kept = jnp.where(
                rank_id < ranks[j, 0, row + i], c[i * half : (i + 1) * half], 0.0
            ).astype(jnp.bfloat16)
            for at, h in enumerate(halves):
                piece = kept[:, at * group_lanes : (at + 1) * group_lanes]
                if own:
                    recv[h, i, slots(m, j, 1)] = piece
                else:
                    send[h, m, i, pl.ds(j * half, half)] = piece

    def first_coefficients(d):
        for block in range(blocks):
            for g in range(max(1, d * near), (d + 1) * near):
                freq_copy(g, 0, block).wait_recv()
        h = partner(mf // near, d, groups)
        b_one = xall[h, :, :, :, columns(0)].reshape(group_lanes, width)
        b_two = swapped(b_one, chunk, 0)
        for k in range(n - 1):
            leading = across(k) if k < n // 2 else k - n // 2 + 1
            trailing = k + 1 if k < n // 2 - 1 else across(k - n // 2 + 1)
            m = inner * leading + (1 - inner) * trailing
            tile_block(m, 0, b_one, b_two, [h], False)
            first_copy(m, d).start()
        tile_block(0, 0, b_one, b_two, [h], True)

    def coefficients(j, leading):
        if not leading:
            for block in range(blocks):
                for g in range(1, nf):
                    freq_copy(g, j, block).wait_recv()
            load_v(j).wait()
        b_one = xall[:, :, :, :, columns(j)].reshape(lanes, width)
        b_two = jnp.concatenate(
            [
                swapped(b_one[h * group_lanes : (h + 1) * group_lanes], chunk, 0)
                for h in range(groups)
            ],
            axis=0,
        )
        if not leading:
            for m in range(n):
                tile_block(m, j, b_one, b_two, range(groups), m == 0)
        for o in range(3):
            load_band_wait(o, j)
        c = product(
            vb[:, j, 0].reshape(3 * half, width), vb[:, j, 1].reshape(3 * half, width), b_one, b_two
        ).astype(jnp.bfloat16)
        for o in range(3):
            cband[o, j + o] = c[o * half : (o + 1) * half]

    def load_band_wait(o, j):
        pltpu.make_async_copy(
            v_hbm.at[0, 0, j, :, pl.ds(half, half), :], vb.at[o, j], sem_vb.at[o, j]
        ).wait()

    for block in range(blocks):
        spectra(0, block)
        if block == 0:
            pl.semaphore_wait(barrier, n + nf - 2)
        share_spectra(0, block)
    if tiles > 2:
        for block in range(blocks):
            for q in range(2):
                load_traces(q, 2, block).start()
    load_v(0).wait()
    first_coefficients(0)
    for block in range(blocks):
        spectra(1, block)
        share_spectra(1, block)
    for d in range(1, groups):
        first_coefficients(d)
    if tiles > 3:
        for block in range(blocks):
            for q in range(2):
                load_traces(q, 3, block).start()
    for j in range(2, tiles):
        load_v(j).start()
    coefficients(0, True)
    band_copy(1).start()
    for m in range(n):
        load_u(m).start()
    for j in range(tiles):
        for o in range(3):
            load_band(o, j, False).start()

    def advance(step, _):
        @pl.when(step < tiles)
        def _():
            for block in range(blocks):
                spectra(step, block)
                share_spectra(step, block)

        @pl.when(step + 2 < tiles)
        def _():
            for block in range(blocks):
                for q in range(2):
                    load_traces(q, step + 2, block).start()

        coefficients(step - 1, False)
        return 0

    lax.fori_loop(2, tiles + 1, advance, 0)

    def send_rows(i, _):
        for h in range(groups):
            for m in range(1, n // 2):
                row_copy(m, i, h).start()
            for k in range(n // 2):
                row_copy(across(k), i, h).start()
        return 0

    band_copy(0).start()
    lax.fori_loop(0, tiles, send_rows, 0)

    for m in range(n):
        load_u(m).wait()
    for j in range(tiles):
        for o in range(3):
            load_band(o, j, False).wait()
    for m in range(1, n):
        for d in range(groups):
            first_copy(m, d).wait_recv()
    band_copy(0).wait_recv()
    band_copy(1).wait_recv()
    zero = jnp.zeros((half, lanes), jnp.bfloat16)
    bin_[0] = jnp.where(first == 0, bin_[0], zero)
    bin_[1] = jnp.where(last == 0, bin_[1], zero)
    cband[2, 0 + 1] = bin_[0]
    cband[0, tiles] = bin_[1]
    gsum[...] = jnp.zeros_like(gsum)

    def transposed(c, u):
        return lax.dot_general(c, u, TN_DIMS, preferred_element_type=jnp.float32)

    def add_source(m, i):
        c = jnp.concatenate([recv[h, i, slots(m, 0, tiles)] for h in range(groups)], axis=1)
        for part in range(2):
            u = u_s[i, pl.ds(m * tiles, tiles), part].reshape(tiles * half, width)
            acc[part] += transposed(c, u)

    def respond(i, _):
        c = jnp.concatenate([cband[o, i + 1] for o in range(3)], axis=0)
        for part in range(2):
            acc[part] = transposed(c, ub[:, i, part].reshape(3 * half, width))
        add_source(0, i)

        def from_peer(m, _):
            for h in range(groups):
                row_copy(m, i, h).wait_recv()
            add_source(m, i)
            return 0

        lax.fori_loop(1, n // 2, from_peer, 0)
        lax.fori_loop(0, n // 2, lambda k, _: from_peer(across(k), _), 0)
        parts = []
        for p, (other, sign) in enumerate(((2, -1), (3, 1), (0, 1), (1, -1))):
            blocks_of = []
            for h in range(groups):
                one = acc[0, pl.ds(h * group_lanes + p * chunk, chunk)]
                two = acc[1, pl.ds(h * group_lanes + other * chunk, chunk)]
                blocks_of.append(one + two if sign > 0 else one - two)
            parts.append(jnp.concatenate(blocks_of, axis=0).astype(jnp.bfloat16))
        for c in range(2):
            minus[0, c, :, columns(i)] = parts[2 * c]
            plus[0, c, :, columns(i)] = parts[2 * c + 1]
        gsum[...] += lax.dot_general(
            jnp.concatenate(parts, axis=0),
            jnp.concatenate([parts[1], parts[3]], axis=0),
            NT_DIMS,
            preferred_element_type=jnp.float32,
        )
        return 0

    lax.fori_loop(0, tiles, respond, 0)

    receivers = total_tiles * width
    share = count // n
    outs = (cross, normal)
    for q, scale in enumerate((1.0 / math.sqrt(receivers), 1.0 / receivers)):
        top = slice(q * count, (q + 1) * count)
        low = slice((2 + q) * count, (3 + q) * count)
        real = (gsum[top, :count] + gsum[low, count:]) * scale
        imag = (gsum[low, :count] - gsum[top, count:]) * scale
        for d in range(n):
            gsend[d, q, 0] = real[d * share : (d + 1) * share].astype(jnp.bfloat16)
            gsend[d, q, 1] = imag[d * share : (d + 1) * share].astype(jnp.bfloat16)
    for m in range(n - 1, 0, -1):
        gram_copy(m).start()
    for q, scale in enumerate((1.0 / math.sqrt(receivers), 1.0 / receivers)):
        mine = pl.ds(pl.multiple_of(q * count + me * share, share), share)
        under = pl.ds(pl.multiple_of((2 + q) * count + me * share, share), share)
        outs[q][0, 0] = (gsum[mine, :count] + gsum[under, count:]) * scale
        outs[q][0, 1] = (gsum[under, :count] - gsum[mine, count:]) * scale
    for m in range(1, n):
        gram_copy(m).wait_recv()
        for q in range(2):
            outs[q][0] += grecv[m, q].astype(jnp.float32)

    for j in range(tiles):
        for block in range(blocks):
            for g in range(1, nf):
                freq_copy(g, j, block).wait_send()
        for m in range(1, n):
            for h in range(groups):
                row_copy(m, j, h).wait_send()
    for m in range(1, n):
        for d in range(groups):
            first_copy(m, d).wait_send()
    band_copy(0).wait_send()
    band_copy(1).wait_send()
    for m in range(1, n):
        gram_copy(m).wait_send()


def hand_over(count, *refs):
    copies = [
        pltpu.make_async_copy(refs[k], refs[count + k], refs[2 * count].at[k]) for k in range(count)
    ]
    for copy in copies:
        copy.start()
    for copy in copies:
        copy.wait()


def on_device(n, nf, plus_time, minus_time, gate_starts, tile_ranks, u_factors, v_factors):
    freq_total = u_factors.shape[0] * nf
    tiles = v_factors.shape[2]
    half = v_factors.shape[4] // 2
    width = v_factors.shape[5]
    sl, samples, receivers = plus_time.shape
    table = gate_table(freq_total, samples)
    sources = math.gcd(16, sl)
    blocks = sl // sources
    rows = freq_total * 2 * sources
    count = sl * nf
    lanes = 4 * count
    share = count // n
    near = math.gcd(nf, 2)
    groups = nf // near
    bf16, f32 = jnp.bfloat16, jnp.float32
    vmem = pl.BlockSpec(memory_space=pltpu.VMEM)
    anywhere = pl.BlockSpec(memory_space=pl.ANY)
    dma = pltpu.SemaphoreType.DMA
    starts = gate_starts.T
    ranks = tile_ranks.transpose(2, 0, 1)
    shapes = (
            jax.ShapeDtypeStruct((1, 2, count, receivers), bf16),
            jax.ShapeDtypeStruct((1, 2, count, receivers), bf16),
            jax.ShapeDtypeStruct((1, 2, share, count), f32),
            jax.ShapeDtypeStruct((1, 2, share, count), f32),
    )
    results = pl.pallas_call(
        functools.partial(operator_kernel, n, nf),
        out_shape=tuple(pltpu.VMEM(shape.shape, shape.dtype) for shape in shapes),
        in_specs=[anywhere] * 7,
        out_specs=(vmem, vmem, vmem, vmem),
        scratch_shapes=[
            pltpu.SMEM(starts.shape, jnp.int32),
            pltpu.SMEM(ranks.shape, jnp.int32),
            pltpu.VMEM(table.shape, f32),
            pltpu.VMEM((rows, 2 * samples), f32),
            pltpu.VMEM((freq_total, 2, 2, sl, receivers), bf16),
            pltpu.VMEM((2, 2, sl, samples, width), bf16),
            pltpu.VMEM((groups, 2, 2, near * sl, receivers), bf16),
            pltpu.VMEM((tiles, n * tiles, 2, half, width), bf16),
            pltpu.VMEM((tiles, n * tiles, 2, half, width), bf16),
            pltpu.VMEM((3, tiles, 2, half, width), bf16),
            pltpu.VMEM((3, tiles, 2, half, width), bf16),
            pltpu.VMEM((groups, n, tiles, tiles * half, lanes // groups), bf16),
            pltpu.VMEM((groups, tiles, n * tiles * half, lanes // groups), bf16),
            pltpu.VMEM((3, tiles + 2, half, lanes), bf16),
            pltpu.VMEM((2, half, lanes), bf16),
            pltpu.VMEM((2, lanes, width), f32),
            pltpu.VMEM((lanes, 2 * count), f32),
            pltpu.VMEM((n, 2, 2, share, count), bf16),
            pltpu.VMEM((n, 2, 2, share, count), bf16),
            dma((3,)),
            dma((2, tiles, blocks)),
            dma((tiles,)),
            dma((n,)),
            dma((3, tiles)),
            dma((3, tiles)),
            dma((nf, tiles, blocks)),
            dma((nf, tiles, blocks)),
            dma((n, groups)),
            dma((n, groups)),
            dma((n, tiles, groups)),
            dma((n, tiles, groups)),
            dma((2,)),
            dma((2,)),
            dma((n,)),
            dma((n,)),
        ],
        compiler_params=pltpu.CompilerParams(
            collective_id=0, has_side_effects=True, vmem_limit_bytes=57 << 20
        ),
        name="reflection_operator",
    )(starts, ranks, table, plus_time, minus_time, u_factors, v_factors)
    return pl.pallas_call(
        functools.partial(hand_over, len(shapes)),
        out_shape=shapes,
        in_specs=[vmem] * len(shapes),
        out_specs=[anywhere] * len(shapes),
        scratch_shapes=[dma((len(shapes),))],
        compiler_params=pltpu.CompilerParams(vmem_limit_bytes=4 << 20),
        name="hand_over",
    )(*results)


def solution(mesh):
    placed = (
        P("freq", None, "tile"),
        P("freq", None, "tile"),
        P("freq", "tile"),
        P("freq", None, "tile"),
        P("freq", "tile", None, None, None, None),
        P("freq", None, "tile", None, None, None),
    )
    return jax.shard_map(
        functools.partial(on_device, mesh.shape["tile"], mesh.shape["freq"]),
        mesh=mesh,
        in_specs=placed,
        out_specs=(
            P("freq", None, None, "tile"),
            P("freq", None, None, "tile"),
            P("freq", None, "tile", None),
            P("freq", None, "tile", None),
        ),
        check_vma=False,
    )
```
